32 devices in a mesh: bx: 8 (over z, x), by: 4 (over y, core).
Axes of the slice: x: 2, y: 2, z: 4, core: 2. Of those that a mesh axis runs over, the one named last changes fastest.
Arguments:
- tokens: bfloat16 [8, 4, 1024, 512], P('bx', 'by'), may hold values from -6 to 6
- norm_gain: float32 [512], replicated, may hold values from 0.1 to 1.9
- w_query_key: bfloat16 [512, 1024], replicated
- w_value: bfloat16 [512, 512], replicated, may hold values from -1 to 1
- w_out: bfloat16 [512, 512], replicated, may hold values from -0.25 to 0.25
- cotangent: bfloat16 [8, 4, 1024, 512], P('bx', 'by'), may hold values from -6 to 6
- block_order: int32 [8, 4, 1024], P('bx', 'by'), may hold values from 0 to 1023, each once within a row
- neighbour_ids: int32 [8, 4, 4, 4], replicated, may hold values from 0 to 127, as said below
- neighbour_count: int32 [8, 4, 4], replicated, may hold values from 1 to 4
Outputs:
- branch_out: bfloat16 [8, 4, 1024, 512], P('bx', 'by')
- grad_tokens: float32 [8, 4, 1024, 512], P('bx', 'by')
- grad_w_query_key: float32 [512, 1024], replicated
- grad_w_value: float32 [512, 512], replicated
- grad_w_out: float32 [512, 512], replicated
- grad_norm_gain: float32 [512], replicated
The draws below stay inside these ranges and needn't reach their ends.
Inputs may be any that keep to these rules, and one draw needn't show every extreme that they name: `neighbour_ids`: block ids are (x * 4 + y) * 4 + b. Entry j < neighbour_count of query block b on brick (x, y) names a block other than b itself, either another block of brick (x, y) or a block of a brick one step away along exactly one axis (x - 1, x + 1, y - 1 or y + 1); the live entries of one list differ. Entries from neighbour_count on hold the query block's own id. Over all query blocks of one brick, at most 2 distinct blocks of any one other brick are named, and every brick names exactly 2 blocks of some other brick. `block_order`: on every brick, a permutation of the arrival rows.
All inputs are finite; a program needn't handle non-finite values.
Results may differ from the reference program's by a relative error of at most 0.006.
The reference program's roundings to bfloat16 on the way count: a program that leaves them out, or rounds other values in their place, can miss the bound.
Values may be sent and summed in bfloat16 or wider, within the bound.
A program may use at most 256 MiB of HBM per device.

```python
import math
import jax
import jax.numpy as jnp
from jax import lax

D = 512
HEADS = 8
BLK = 256
NB = 4
CAP = 2
BLK_DEV = 4
TOK_DEV = 1024
BRICKS_X = 8
BRICKS_Y = 4


def neighbour_tables(key):
    base_key = jax.random.fold_in(key, 7)
    key_offer, key_score, key_first, key_second = jax.random.split(base_key, 4)
    grid_x = jnp.arange(BRICKS_X, dtype=jnp.int32)[:, None, None]
    grid_y = jnp.arange(BRICKS_Y, dtype=jnp.int32)[None, :, None]
    step_x = jnp.array([-1, 1, 0, 0], dtype=jnp.int32)
    step_y = jnp.array([0, 0, -1, 1], dtype=jnp.int32)
    near_x, near_y = jnp.broadcast_arrays(grid_x + step_x, grid_y + step_y)
    inside = (near_x >= 0) & (near_x < BRICKS_X) & (near_y >= 0) & (near_y < BRICKS_Y)
    near_brick = jnp.clip(near_x, 0, BRICKS_X - 1) * BRICKS_Y + jnp.clip(near_y, 0, BRICKS_Y - 1)
    block_range = jnp.arange(BLK_DEV, dtype=jnp.int32)
    offer_scores = jax.random.randint(key_offer, (BRICKS_X, BRICKS_Y, 4, BLK_DEV), 0, 1 << 20) * BLK_DEV + block_range
    offered = jnp.argsort(offer_scores, axis=-1, stable=True)[..., :CAP].astype(jnp.int32)
    offer_ids = (near_brick[..., None] * BLK_DEV + offered).reshape(BRICKS_X, BRICKS_Y, 4 * CAP)
    offer_fine = jnp.repeat(inside, CAP, axis=-1)
    own_brick = grid_x[..., 0] * BRICKS_Y + grid_y[..., 0]
    own_ids = own_brick[..., None] * BLK_DEV + block_range
    columns = BLK_DEV + 4 * CAP
    candidates = jnp.concatenate([jnp.broadcast_to(own_ids[:, :, None, :], (BRICKS_X, BRICKS_Y, BLK_DEV, BLK_DEV)), jnp.broadcast_to(offer_ids[:, :, None, :], (BRICKS_X, BRICKS_Y, BLK_DEV, 4 * CAP))], axis=-1)
    candidate_fine = jnp.concatenate([jnp.broadcast_to(block_range[:, None] != block_range[None, :], (BRICKS_X, BRICKS_Y, BLK_DEV, BLK_DEV)), jnp.broadcast_to(offer_fine[:, :, None, :], (BRICKS_X, BRICKS_Y, BLK_DEV, 4 * CAP))], axis=-1)
    column_range = jnp.arange(columns, dtype=jnp.int32)
    scores = jax.random.randint(key_score, (BRICKS_X, BRICKS_Y, BLK_DEV, columns), 0, 1 << 20) * columns + column_range
    forced_dir = jnp.where(jnp.arange(BRICKS_X, dtype=jnp.int32) < BRICKS_X - 1, 1, 0)[:, None, None, None]
    forced = (block_range[:, None] == 0) & (column_range >= BLK_DEV) & ((column_range - BLK_DEV) // CAP == forced_dir)
    scores = jnp.where(forced, scores + (1 << 26), scores)
    scores = jnp.where(candidate_fine, scores, -1 - column_range)
    _, picked = lax.top_k(scores, NB)
    chosen = jnp.take_along_axis(candidates, picked, axis=-1)
    first_count = jax.random.randint(key_first, (BRICKS_X, BRICKS_Y, BLK_DEV), 1, NB + 1)
    second_count = jax.random.randint(key_second, (BRICKS_X, BRICKS_Y, BLK_DEV), 1, NB + 1)
    counts = jnp.maximum(first_count, second_count)
    counts = jnp.where(block_range == 0, NB, jnp.where(block_range == BLK_DEV - 1, 1, counts))
    listed = jnp.where(jnp.arange(NB, dtype=jnp.int32) < counts[..., None], chosen, own_ids[..., None])
    return (listed.astype(jnp.int32), counts.astype(jnp.int32))


def draw_neighbour_ids(key, part):
    listed, _ = neighbour_tables(key)
    return listed


def draw_neighbour_count(key, part):
    _, counts = neighbour_tables(key)
    return counts


def draw_tokens(key, part):
    row_shape = (BRICKS_X, BRICKS_Y, TOK_DEV, D)
    key_base = jax.random.fold_in(jax.random.fold_in(key, 5), 0)
    key_scale = jax.random.fold_in(jax.random.fold_in(key, 5), 2)
    row_scale = jnp.exp(jax.random.uniform(key_scale, (BRICKS_X, BRICKS_Y, TOK_DEV, 1), jnp.float32, -1.0, 1.0))
    token_rows = jax.random.normal(key_base, row_shape, jnp.float32) * row_scale
    return jnp.clip(token_rows, -6.0, 6.0).astype(jnp.bfloat16)


def draw_w_query_key(key, part):
    key_query, key_key = jax.random.split(jax.random.fold_in(key, 11), 2)
    spread = D ** (-0.5)
    w_query = jax.random.normal(key_query, (D, D), jnp.float32) * spread
    w_key = jax.random.normal(key_key, (D, D), jnp.float32) * spread
    return jnp.concatenate([w_query, w_key], axis=1).astype(jnp.bfloat16)


def shard_levels(key, shape, cuts, least, largest):
    def one(dim, shards_of):
        steps = jax.random.uniform(jax.random.fold_in(jax.random.fold_in(key, 6), dim), (shards_of,), jnp.float32, least / len(cuts), largest / len(cuts))
        return jnp.repeat(jnp.exp(steps), shape[dim] // shards_of).reshape((-1,) + (1,) * (len(shape) - dim - 1))

    gain = one(*cuts[0])
    for cut in cuts[1:]:
        gain = gain * one(*cut)
    return gain


def noise(rng, dims, scale, bound, pieces=(), held_as=jnp.bfloat16):
    gain = shard_levels(rng, dims, pieces, -0.22, 0.18) if pieces else 1.0
    values = jax.random.normal(rng, dims, jnp.float32) * scale * gain
    return jnp.minimum(jnp.maximum(values, -bound), bound).astype(held_as)


def setup_inputs(seed: int = 0) -> dict:
    arg_keys = jax.random.split(jax.random.key(seed), 10)
    tokens = draw_tokens(jax.random.fold_in(arg_keys[9], 71), 0)
    norm_gain = jnp.clip(1.0 + 0.18 * jax.random.normal(arg_keys[1], (D,), jnp.float32), 0.1, 1.9)
    w_query_key = draw_w_query_key(jax.random.fold_in(arg_keys[9], 71), 0)
    w_value = noise(arg_keys[3], (D, D), (D // 16) ** -0.5, 1.0)
    w_out = noise(arg_keys[4], (D, D), D ** -0.5, 0.25)
    cotangent = noise(arg_keys[5], (BRICKS_X, BRICKS_Y, TOK_DEV, D), 1.0, 6.0, ((0, 8), (1, 4)))
    block_order = jax.vmap(lambda own: jax.random.permutation(own, TOK_DEV))(jax.random.split(arg_keys[6], BRICKS_X * BRICKS_Y)).reshape((BRICKS_X, BRICKS_Y, TOK_DEV)).astype(jnp.int32)
    neighbour_ids = draw_neighbour_ids(jax.random.fold_in(arg_keys[9], 71), 0)
    neighbour_count = draw_neighbour_count(jax.random.fold_in(arg_keys[9], 71), 0)
    return dict(tokens=tokens, norm_gain=norm_gain, w_query_key=w_query_key, w_value=w_value, w_out=w_out, cotangent=cotangent, block_order=block_order, neighbour_ids=neighbour_ids, neighbour_count=neighbour_count)


EPSILON = 1e-06

def rms_rows(token_rows, gain_row):
    values = token_rows.astype(jnp.float32)
    inv_rms = lax.rsqrt(lax.optimization_barrier(jnp.mean(values * values, axis=-1, keepdims=True)) + EPSILON)
    return (values, inv_rms, (values * inv_rms * gain_row).astype(jnp.bfloat16))

def attend_block(query_rows, key_value_rows, live_cols, grad_context):
    features = query_rows.shape[-1]
    head_size = features // HEADS
    row_count = query_rows.shape[0]
    factor = 1.0 / math.sqrt(head_size)
    highest = lax.Precision.HIGHEST
    queries = query_rows.reshape(row_count, HEADS, head_size).astype(jnp.float32)
    kv_rows = key_value_rows.reshape(-1, 2 * features)
    key_rows = kv_rows[:, :features].reshape(-1, HEADS, head_size).astype(jnp.float32)
    value_rows = kv_rows[:, features:].reshape(-1, HEADS, head_size).astype(jnp.float32)
    grad_rows = grad_context.reshape(row_count, HEADS, head_size).astype(jnp.float32)
    scores = jnp.einsum('ihd,jhd->hij', queries, key_rows, precision=highest) * factor
    scores = jnp.where(live_cols[None, None, :], scores, -1e+30)
    row_max = lax.optimization_barrier(jnp.max(scores, axis=-1, keepdims=True))
    powers = jnp.exp(scores - row_max)
    attn_probs = powers / lax.optimization_barrier(jnp.sum(powers, axis=-1, keepdims=True))
    probs_low = attn_probs.astype(jnp.bfloat16)
    context = jnp.einsum('hij,jhd->ihd', probs_low.astype(jnp.float32), value_rows, precision=highest).astype(jnp.bfloat16)
    grad_probs = jnp.einsum('ihd,jhd->hij', grad_rows, value_rows, precision=highest)
    centre = lax.optimization_barrier(jnp.sum(attn_probs * grad_probs, axis=-1, keepdims=True))
    grad_scores = (attn_probs * (grad_probs - centre) * factor).astype(jnp.bfloat16)
    grad_query = jnp.einsum('hij,jhd->ihd', grad_scores.astype(jnp.float32), key_rows, precision=highest).astype(jnp.bfloat16)
    grad_keys = jnp.einsum('hij,ihd->jhd', grad_scores.astype(jnp.float32), queries, precision=highest)
    grad_values = jnp.einsum('hij,ihd->jhd', probs_low.astype(jnp.float32), grad_rows, precision=highest)
    slots = key_value_rows.shape[0]
    return (context.reshape(row_count, features), grad_query.reshape(row_count, features), grad_keys.reshape(slots, row_count, features), grad_values.reshape(slots, row_count, features))

def reference(tokens, norm_gain, w_query_key, w_value, w_out, cotangent, block_order, neighbour_ids, neighbour_count):
    bricks = BRICKS_X * BRICKS_Y
    features = D
    row_order = block_order.reshape(bricks, TOK_DEV)
    sorted_rows = jnp.take_along_axis(tokens.reshape(bricks, TOK_DEV, features), row_order[:, :, None], axis=1).reshape(-1, features)
    sorted_grad = jnp.take_along_axis(cotangent.reshape(bricks, TOK_DEV, features), row_order[:, :, None], axis=1).reshape(-1, features)
    values, inv_rms, normed = rms_rows(sorted_rows, norm_gain)
    query_rows = jnp.dot(normed, w_query_key[:, :features], preferred_element_type=jnp.float32).astype(jnp.bfloat16)
    w_pair = jnp.concatenate([w_query_key[:, features:], w_value], axis=1)
    key_value = jnp.dot(normed, w_pair, preferred_element_type=jnp.float32).astype(jnp.bfloat16)
    key_value = key_value.reshape(bricks * BLK_DEV, BLK, 2 * features)
    d_context = jnp.dot(sorted_grad, w_out.T, preferred_element_type=jnp.float32).astype(jnp.bfloat16)
    all_ids = neighbour_ids.reshape(bricks, BLK_DEV, NB)
    all_counts = neighbour_count.reshape(bricks, BLK_DEV)
    query_blocks = query_rows.reshape(bricks, BLK_DEV, BLK, features)
    grad_blocks = d_context.reshape(bricks, BLK_DEV, BLK, features)
    entries = BLK_DEV * (NB + 1)

    def per_block(block_item):
        block_query, block_grad, key_ids, live_slots = block_item
        live_cols = jnp.repeat(live_slots, BLK)
        return attend_block(block_query, key_value[key_ids], live_cols, block_grad)

    def per_brick(grad_total, brick_item):
        brick, brick_query, brick_grad, brick_ids, brick_count = brick_item
        own_ids = brick * BLK_DEV + jnp.arange(BLK_DEV, dtype=jnp.int32)
        key_ids = jnp.concatenate([own_ids[:, None], brick_ids.astype(jnp.int32)], axis=1)
        live_slots = jnp.concatenate([jnp.ones((BLK_DEV, 1), dtype=jnp.bool_), jnp.arange(NB, dtype=jnp.int32)[None, :] < brick_count[:, None]], axis=1)
        context, grad_query, key_terms, value_terms = lax.map(per_block, (brick_query, brick_grad, key_ids, live_slots))
        flat_ids = key_ids.reshape(entries)
        flat_terms = jnp.concatenate([key_terms, value_terms], axis=-1).reshape(entries, BLK * 2 * features)
        same_block = (flat_ids[:, None] == flat_ids[None, :]).astype(jnp.float32)
        summed = jnp.dot(same_block, flat_terms, precision=lax.Precision.HIGHEST)
        earlier = lax.optimization_barrier(jnp.sum(jnp.tril(same_block, -1), axis=1))
        owned = flat_ids // BLK_DEV == brick
        shipped = lax.optimization_barrier(summed.astype(jnp.bfloat16)).astype(jnp.float32)
        partial_sums = jnp.where(owned[:, None], summed, shipped)
        partial_sums = jnp.where((earlier == 0)[:, None], partial_sums, jnp.zeros_like(partial_sums))
        grad_total = grad_total.at[flat_ids].add(partial_sums.reshape(entries, BLK, 2 * features))
        return (grad_total, (context, grad_query))
    start_total = jnp.zeros((bricks * BLK_DEV, BLK, 2 * features), jnp.float32)
    grad_total, (context, grad_query) = lax.scan(per_brick, start_total, (jnp.arange(bricks, dtype=jnp.int32), query_blocks, grad_blocks, all_ids, all_counts))
    grad_kv = grad_total.astype(jnp.bfloat16).reshape(-1, 2 * features)
    context = context.reshape(-1, features)
    grad_query = grad_query.reshape(-1, features)
    out_rows = jnp.dot(context, w_out, preferred_element_type=jnp.float32).astype(jnp.bfloat16)
    grad_w_out = jnp.dot(context.T, sorted_grad, preferred_element_type=jnp.float32)
    grad_proj = jnp.concatenate([grad_query, grad_kv], axis=1)
    w_all = jnp.concatenate([w_query_key, w_value], axis=1)
    grad_normed = jnp.dot(grad_proj, w_all.T, preferred_element_type=jnp.float32)
    grad_all = jnp.dot(normed.T, grad_proj, preferred_element_type=jnp.float32)
    grad_norm_gain = lax.optimization_barrier(jnp.sum(grad_normed * (values * inv_rms), axis=0))
    scaled_grad = grad_normed * norm_gain
    grad_rows = inv_rms * scaled_grad - values * (inv_rms * inv_rms * inv_rms) * lax.optimization_barrier(jnp.mean(values * scaled_grad, axis=-1, keepdims=True))
    inverse = jnp.argsort(row_order, axis=1).astype(jnp.int32)
    branch_out = jnp.take_along_axis(out_rows.reshape(bricks, TOK_DEV, features), inverse[:, :, None], axis=1)
    grad_tokens = jnp.take_along_axis(grad_rows.reshape(bricks, TOK_DEV, features), inverse[:, :, None], axis=1)
    return (branch_out.reshape(BRICKS_X, BRICKS_Y, TOK_DEV, features), grad_tokens.reshape(BRICKS_X, BRICKS_Y, TOK_DEV, features), grad_all[:, :2 * features], grad_all[:, 2 * features:], grad_w_out, grad_norm_gain)
```

```python
import functools
import math

import jax
import jax.numpy as jnp
from jax import lax
from jax.experimental import pallas as pl
from jax.experimental.pallas import tpu as pltpu
from jax.sharding import PartitionSpec as P

HEADS = 8
BLK = 256
CAP = 2


EPSILON = 1e-06


def from_behind(block, axis, distance):
    devices = range(lax.axis_size(axis))
    route = [(i - distance, i) for i in devices if i - distance in devices]
    return lax.ppermute(block, axis, route)


def rms_rows(token_rows, gain_row):
    values = token_rows.astype(jnp.float32)
    inv_rms = lax.rsqrt(jnp.mean(values * values, axis=-1, keepdims=True) + EPSILON)
    return (values, inv_rms, (values * inv_rms * gain_row).astype(jnp.bfloat16))


def attend_kernel(
    index_ref,
    live_ref,
    q_ref,
    g_ref,
    kv_ref,
    xp_ref,
    xm_ref,
    yp_ref,
    ym_ref,
    ctx_ref,
    dq_ref,
    own_ref,
    away_ref,
    pool,
    turned,
    total,
    scores,
    slopes,
    *,
    factor,
):
    block = pl.program_id(1)
    blocks = kv_ref.shape[0]
    side = xp_ref.shape[0]
    pool_rows = pool.shape[0]
    slots = scores.shape[0]
    lanes = q_ref.shape[1]
    half = lanes // 2

    @pl.when(block == 0)
    def _():
        for i in range(blocks):
            pool[i] = kv_ref[i]
        for s, ref in enumerate((xp_ref, xm_ref, yp_ref, ym_ref)):
            for i in range(side):
                pool[blocks + s * side + i] = ref[i]
        for i in range(pool_rows):
            turned[i] = pool[i].T
            total[i] = jnp.zeros(total.shape[1:], jnp.float32)

    query = q_ref[...] * jnp.asarray(factor, jnp.bfloat16)
    grad = g_ref[...]
    query_t = query.T
    grad_t = grad.T
    zero_t = jnp.zeros((half, query.shape[0]), jnp.bfloat16)
    lane = lax.broadcasted_iota(jnp.int32, (1, lanes), 1)
    ctx_parts = []
    dq_parts = []
    for h in range(2):
        mine = lane < half if h == 0 else lane >= half
        q_h = jnp.where(mine, query, jnp.zeros_like(query))
        g_h = jnp.where(mine, grad, jnp.zeros_like(grad))
        rows = slice(h * half, (h + 1) * half)
        order = (lambda t: [t, zero_t]) if h == 0 else (lambda t: [zero_t, t])
        qt_h = jnp.concatenate(order(query_t[rows]), axis=0)
        gt_h = jnp.concatenate(order(grad_t[rows]), axis=0)
        top = None
        for j in range(slots):
            k_j = pool[index_ref[block, j], :, :lanes]
            s_j = jnp.dot(k_j, qt_h, preferred_element_type=jnp.float32)
            scores[j] = s_j
            m_j = jnp.max(s_j, axis=0, keepdims=True)
            if j:
                m_j = jnp.where(live_ref[block, j] > 0, m_j, -1e30)
            top = m_j if top is None else jnp.maximum(top, m_j)
            v_j = pool[index_ref[block, j], :, lanes:]
            slopes[j] = jnp.dot(v_j, gt_h, preferred_element_type=jnp.float32)
        norm = None
        for j in range(slots):
            base = top
            if j:
                base = jnp.where(live_ref[block, j] > 0, top, 1e30)
            e_j = jnp.exp(scores[j] - base)
            scores[j] = e_j
            n_j = jnp.sum(e_j, axis=0, keepdims=True)
            c_j = jnp.sum(e_j * slopes[j], axis=0, keepdims=True)
            norm = n_j if norm is None else norm + n_j
            centre = c_j if j == 0 else centre + c_j
        inverse = 1.0 / norm
        centre = centre * inverse
        ctx_t = None
        for j in range(slots):
            p_j = scores[j] * inverse
            low = p_j.astype(jnp.bfloat16)
            d_j = (p_j * (slopes[j] - centre)).astype(jnp.bfloat16)
            at = index_ref[block, j]
            k_t = turned[at, h * half : (h + 1) * half, :]
            v_t = turned[at, lanes + h * half : lanes + (h + 1) * half, :]
            c_t = jnp.dot(v_t, low, preferred_element_type=jnp.float32)
            t_t = jnp.dot(k_t, d_j, preferred_element_type=jnp.float32)
            ctx_t = c_t if j == 0 else ctx_t + c_t
            dq_t = t_t if j == 0 else dq_t + t_t
            total[at, :, :lanes] += jnp.dot(d_j, q_h, preferred_element_type=jnp.float32)
            total[at, :, lanes:] += jnp.dot(low, g_h, preferred_element_type=jnp.float32)
        ctx_parts.append(ctx_t)
        dq_parts.append(dq_t * factor)
    ctx_ref[...] = jnp.concatenate(ctx_parts, axis=0).T.astype(jnp.bfloat16)
    dq_ref[...] = jnp.concatenate(dq_parts, axis=0).T.astype(jnp.bfloat16)

    @pl.when(block == pl.num_programs(1) - 1)
    def _():
        for i in range(blocks):
            own_ref[i] = total[i]
        for i in range(blocks, pool_rows):
            away_ref[i - blocks] = total[i].astype(jnp.bfloat16)


def attend(key_index, live_keys, query_rows, d_context, key_value, fetched):
    row_count, features = query_rows.shape
    blocks, blk, wide = key_value.shape
    side = fetched[0].shape[0]
    pool_rows = blocks + 4 * side
    slots = key_index.shape[1]
    lanes = 2 * features // HEADS
    pairs = HEADS // 2
    factor = 1.0 / math.sqrt(features // HEADS)
    row_spec = pl.BlockSpec((blk, lanes), lambda hp, b, *_: (b, hp))

    def kv_spec(count):
        return pl.BlockSpec((count, blk, 2 * lanes), lambda hp, b, *_: (0, 0, hp))

    return pl.pallas_call(
        functools.partial(attend_kernel, factor=factor),
        grid_spec=pltpu.PrefetchScalarGridSpec(
            num_scalar_prefetch=2,
            grid=(pairs, blocks),
            in_specs=[row_spec, row_spec, kv_spec(blocks)] + [kv_spec(side)] * 4,
            out_specs=[row_spec, row_spec, kv_spec(blocks), kv_spec(4 * side)],
            scratch_shapes=[
                pltpu.VMEM((pool_rows, blk, 2 * lanes), jnp.bfloat16),
                pltpu.VMEM((pool_rows, 2 * lanes, blk), jnp.bfloat16),
                pltpu.VMEM((pool_rows, blk, 2 * lanes), jnp.float32),
                pltpu.VMEM((slots, blk, blk), jnp.float32),
                pltpu.VMEM((slots, blk, blk), jnp.float32),
            ],
        ),
        out_shape=[
            jax.ShapeDtypeStruct((row_count, features), jnp.bfloat16),
            jax.ShapeDtypeStruct((row_count, features), jnp.bfloat16),
            jax.ShapeDtypeStruct((blocks, blk, wide), jnp.float32),
            jax.ShapeDtypeStruct((4 * side, blk, wide), jnp.bfloat16),
        ],
        compiler_params=pltpu.CompilerParams(
            dimension_semantics=("arbitrary", "arbitrary"), vmem_limit_bytes=48 << 20
        ),
        name="attend",
    )(key_index, live_keys, query_rows, d_context, key_value, *fetched)


def weave(left, right):
    rows, features = left.shape
    pairs = HEADS // 2
    both = jnp.stack(
        [left.reshape(rows, pairs, features // pairs), right.reshape(rows, pairs, features // pairs)],
        axis=2,
    )
    return both.reshape(rows, 2 * features)


def shards(
    tokens,
    norm_gain,
    w_query_key,
    w_value,
    w_out,
    cotangent,
    block_order,
    neighbour_ids,
    neighbour_count,
):
    row_count = tokens.shape[2]
    features = tokens.shape[3]
    blocks = row_count // BLK
    slot_count = neighbour_ids.shape[3]
    extent_x = lax.axis_size("bx")
    extent_y = lax.axis_size("by")
    brick_x = lax.axis_index("bx")
    brick_y = lax.axis_index("by")
    my_brick = brick_x * extent_y + brick_y
    row_order = block_order[0, 0]
    arrival_grad = cotangent[0, 0]
    values, inv_rms, arrival_normed = rms_rows(tokens[0, 0], norm_gain)
    order_mask = (
        row_order[:, None] == lax.broadcasted_iota(jnp.int32, (row_count, row_count), 1)
    ).astype(jnp.bfloat16)
    normed = jnp.dot(order_mask, arrival_normed, preferred_element_type=jnp.float32).astype(
        jnp.bfloat16
    )
    sorted_grad = jnp.dot(order_mask, arrival_grad, preferred_element_type=jnp.float32).astype(
        jnp.bfloat16
    )
    query_rows = jnp.dot(
        normed, w_query_key[:, :features], preferred_element_type=jnp.float32
    ).astype(jnp.bfloat16)
    w_pair = weave(w_query_key[:, features:], w_value)
    key_value = jnp.dot(normed, w_pair, preferred_element_type=jnp.float32).astype(jnp.bfloat16)
    key_value = key_value.reshape(blocks, BLK, 2 * features)
    d_context = lax.dot_general(
        sorted_grad, w_out, (((1,), (1,)), ((), ())), preferred_element_type=jnp.float32
    ).astype(jnp.bfloat16)
    slot_range = jnp.arange(slot_count, dtype=jnp.int32)
    block_range = jnp.arange(blocks, dtype=jnp.int32)
    side_range = jnp.arange(1, 5, dtype=jnp.int32)
    my_ids = neighbour_ids[brick_x, brick_y]
    my_count = neighbour_count[brick_x, brick_y]
    live_slots = slot_range[None, :] < my_count[:, None]
    owner_brick = my_ids // blocks
    offset = my_ids % blocks
    delta_x = owner_brick // extent_y - brick_x
    delta_y = owner_brick % extent_y - brick_y
    segment = jnp.where(
        delta_x == -1,
        1,
        jnp.where(delta_x == 1, 2, jnp.where(delta_y == -1, 3, jnp.where(delta_y == 1, 4, 0))),
    )

    def selection_for(req_x, req_y):
        safe_x = jnp.clip(req_x, 0, extent_x - 1)
        safe_y = jnp.clip(req_y, 0, extent_y - 1)
        req_ids = neighbour_ids[safe_x, safe_y]
        req_count = neighbour_count[safe_x, safe_y]
        req_live = slot_range[None, :] < req_count[:, None]
        from_me = req_live & (req_ids // blocks == my_brick)
        wanted = jnp.any(
            from_me[:, :, None] & ((req_ids % blocks)[:, :, None] == block_range), axis=(0, 1)
        )
        ranks = jnp.cumsum(wanted.astype(jnp.int32)) - 1
        pick_rows = wanted[None, :] & (ranks[None, :] == jnp.arange(CAP, dtype=jnp.int32)[:, None])
        return pick_rows.astype(jnp.bfloat16)

    choosers = {}
    for shift_step in (1, -1):
        choosers["bx", shift_step] = selection_for(brick_x + shift_step, brick_y)
        choosers["by", shift_step] = selection_for(brick_x, brick_y + shift_step)
    side_match = (segment[:, :, None, None] == side_range[None, None, :, None]) & (
        offset[:, :, None, None] == block_range[None, None, None, :]
    )
    wanted_here = jnp.any(live_slots[:, :, None, None] & side_match, axis=(0, 1))
    side_ranks = jnp.cumsum(wanted_here.astype(jnp.int32), axis=1) - 1
    rank_of = jnp.sum(jnp.where(side_match, side_ranks[None, None, :, :], 0), axis=(2, 3))
    entry_index = jnp.where(segment == 0, offset, blocks + (segment - 1) * CAP + rank_of)

    def outgoing(source, side_key):
        picked = jnp.einsum(
            "co,otf->ctf", choosers[side_key], source, preferred_element_type=jnp.float32
        )
        return picked.astype(jnp.bfloat16)

    def incoming(returned, side_key):
        return jnp.einsum(
            "co,ctf->otf", choosers[side_key], returned, preferred_element_type=jnp.float32
        )

    fetched = {}
    for shift_step in (1, -1):
        fetched["bx", shift_step] = from_behind(
            outgoing(key_value, ("bx", shift_step)), "bx", shift_step
        )
    for shift_step in (1, -1):
        fetched["by", shift_step] = from_behind(
            outgoing(key_value, ("by", shift_step)), "by", shift_step
        )
    key_index = jnp.concatenate([block_range[:, None], entry_index], axis=1)
    live_keys = jnp.concatenate([jnp.ones((blocks, 1), dtype=jnp.bool_), live_slots], axis=1)
    context, grad_query, own_grad, away_grad = attend(
        key_index,
        live_keys.astype(jnp.int32),
        query_rows,
        d_context,
        key_value,
        [fetched["bx", 1], fetched["bx", -1], fetched["by", 1], fetched["by", -1]],
    )
    returned = {}
    for index, (axis, shift_step) in enumerate((("bx", 1), ("bx", -1), ("by", 1), ("by", -1))):
        returned[axis, shift_step] = from_behind(
            away_grad[index * CAP : (index + 1) * CAP], axis, -shift_step
        )

    def unsort(rows):
        return lax.dot_general(
            order_mask, rows, (((0,), (0,)), ((), ())), preferred_element_type=jnp.float32
        ).astype(jnp.bfloat16)

    context = unsort(context)
    branch_out = jnp.dot(context, w_out, preferred_element_type=jnp.float32).astype(jnp.bfloat16)
    grad_out_part = lax.dot_general(
        context, arrival_grad, (((0,), (0,)), ((), ())), preferred_element_type=jnp.float32
    )
    grad_query = unsort(grad_query)
    grad_q_part = lax.dot_general(
        arrival_normed, grad_query, (((0,), (0,)), ((), ())), preferred_element_type=jnp.float32
    )
    grad_output, grad_q = lax.psum((grad_out_part, grad_q_part), ("bx", "by"))
    for side_key, rows in returned.items():
        own_grad = own_grad + incoming(rows, side_key)
    grad_kv = unsort(own_grad.astype(jnp.bfloat16).reshape(row_count, 2 * features))
    grad_normed = lax.dot_general(
        grad_query,
        w_query_key[:, :features],
        (((1,), (1,)), ((), ())),
        preferred_element_type=jnp.float32,
    ) + lax.dot_general(
        grad_kv, w_pair, (((1,), (1,)), ((), ())), preferred_element_type=jnp.float32
    )
    grad_kv_part = lax.dot_general(
        arrival_normed, grad_kv, (((0,), (0,)), ((), ())), preferred_element_type=jnp.float32
    )
    gain_part = jnp.sum(grad_normed * (values * inv_rms), axis=0)
    grad_kv_sum, grad_gain = lax.psum((grad_kv_part, gain_part), ("bx", "by"))
    scaled_grad = grad_normed * norm_gain
    grad_rows = inv_rms * scaled_grad - values * (inv_rms * inv_rms * inv_rms) * jnp.mean(
        values * scaled_grad, axis=-1, keepdims=True
    )
    pairs = HEADS // 2
    split = grad_kv_sum.reshape(features, pairs, 2, features // pairs)
    grad_key = split[:, :, 0].reshape(features, features)
    grad_val = split[:, :, 1].reshape(features, features)
    grad_qk = jnp.concatenate([grad_q, grad_key], axis=1)
    return (
        branch_out[None, None],
        grad_rows[None, None],
        grad_qk,
        grad_val,
        grad_output,
        grad_gain,
    )


def solution(mesh):
    placed = (
        P("bx", "by", None, None),
        P(),
        P(),
        P(),
        P(),
        P("bx", "by", None, None),
        P("bx", "by", None),
        P(),
        P(),
    )
    return jax.shard_map(
        shards,
        mesh=mesh,
        in_specs=placed,
        out_specs=(P("bx", "by", None, None), P("bx", "by", None, None), P(), P(), P(), P()),
        check_vma=False,
    )
```

```python
import functools
import math

import jax
import jax.numpy as jnp
from jax import lax
from jax.experimental import pallas as pl
from jax.experimental.pallas import tpu as pltpu
from jax.sharding import PartitionSpec as P

HEADS = 8
BLK = 256
CAP = 2


EPSILON = 1e-06


def from_behind(block, axis, distance):
    devices = range(lax.axis_size(axis))
    route = [(i - distance, i) for i in devices if i - distance in devices]
    return lax.ppermute(block, axis, route)


def rms_rows(token_rows, gain_row):
    values = token_rows.astype(jnp.float32)
    inv_rms = lax.rsqrt(jnp.mean(values * values, axis=-1, keepdims=True) + EPSILON)
    return (values, inv_rms, (values * inv_rms * gain_row).astype(jnp.bfloat16))


def attend_kernel(
    index_ref,
    live_ref,
    q_ref,
    g_ref,
    kv_ref,
    xp_ref,
    xm_ref,
    yp_ref,
    ym_ref,
    ctx_ref,
    dq_ref,
    own_ref,
    away_ref,
    pool,
    turned,
    total,
    scores,
    slopes,
    *,
    factor,
):
    block = pl.program_id(1)
    blocks = kv_ref.shape[0]
    side = xp_ref.shape[0]
    pool_rows = pool.shape[0]
    slots = scores.shape[0]
    lanes = q_ref.shape[1]
    half = lanes // 2

    @pl.when(block == 0)
    def _():
        for i in range(blocks):
            pool[i] = kv_ref[i]
        for s, ref in enumerate((xp_ref, xm_ref, yp_ref, ym_ref)):
            for i in range(side):
                pool[blocks + s * side + i] = ref[i]
        for i in range(pool_rows):
            turned[i] = pool[i].T
            total[i] = jnp.zeros(total.shape[1:], jnp.float32)

    query = q_ref[...] * jnp.asarray(factor, jnp.bfloat16)
    grad = g_ref[...]
    query_t = query.T
    grad_t = grad.T
    zero_t = jnp.zeros((half, query.shape[0]), jnp.bfloat16)
    lane = lax.broadcasted_iota(jnp.int32, (1, lanes), 1)
    ctx_parts = []
    dq_parts = []
    for h in range(2):
        mine = lane < half if h == 0 else lane >= half
        q_h = jnp.where(mine, query, jnp.zeros_like(query))
        g_h = jnp.where(mine, grad, jnp.zeros_like(grad))
        rows = slice(h * half, (h + 1) * half)
        order = (lambda t: [t, zero_t]) if h == 0 else (lambda t: [zero_t, t])
        qt_h = jnp.concatenate(order(query_t[rows]), axis=0)
        gt_h = jnp.concatenate(order(grad_t[rows]), axis=0)
        top = None
        for j in range(slots):
            k_j = pool[index_ref[block, j], :, :lanes]
            s_j = jnp.dot(k_j, qt_h, preferred_element_type=jnp.float32)
            scores[j] = s_j
            m_j = jnp.max(s_j, axis=0, keepdims=True)
            if j:
                m_j = jnp.where(live_ref[block, j] > 0, m_j, -1e30)
            top = m_j if top is None else jnp.maximum(top, m_j)
            v_j = pool[index_ref[block, j], :, lanes:]
            slopes[j] = jnp.dot(v_j, gt_h, preferred_element_type=jnp.float32)
        norm = None
        for j in range(slots):
            base = top
            if j:
                base = jnp.where(live_ref[block, j] > 0, top, 1e30)
            e_j = jnp.exp(scores[j] - base)
            scores[j] = e_j
            n_j = jnp.sum(e_j, axis=0, keepdims=True)
            c_j = jnp.sum(e_j * slopes[j], axis=0, keepdims=True)
            norm = n_j if norm is None else norm + n_j
            centre = c_j if j == 0 else centre + c_j
        inverse = 1.0 / norm
        centre = centre * inverse
        ctx_t = None
        for j in range(slots):
            p_j = scores[j] * inverse
            low = p_j.astype(jnp.bfloat16)
            d_j = (p_j * (slopes[j] - centre)).astype(jnp.bfloat16)
            at = index_ref[block, j]
            k_t = turned[at, h * half : (h + 1) * half, :]
            v_t = turned[at, lanes + h * half : lanes + (h + 1) * half, :]
            c_t = jnp.dot(v_t, low, preferred_element_type=jnp.float32)
            t_t = jnp.dot(k_t, d_j, preferred_element_type=jnp.float32)
            ctx_t = c_t if j == 0 else ctx_t + c_t
            dq_t = t_t if j == 0 else dq_t + t_t
            total[at, :, :lanes] += jnp.dot(d_j, q_h, preferred_element_type=jnp.float32)
            total[at, :, lanes:] += jnp.dot(low, g_h, preferred_element_type=jnp.float32)
        ctx_parts.append(ctx_t)
        dq_parts.append(dq_t * factor)
    ctx_ref[...] = jnp.concatenate(ctx_parts, axis=0).T.astype(jnp.bfloat16)
    dq_ref[...] = jnp.concatenate(dq_parts, axis=0).T.astype(jnp.bfloat16)

    @pl.when(block == pl.num_programs(1) - 1)
    def _():
        for i in range(blocks):
            own_ref[i] = total[i]
        for i in range(blocks, pool_rows):
            away_ref[i - blocks] = total[i].astype(jnp.bfloat16)


def attend(key_index, live_keys, query_rows, d_context, key_value, fetched):
    row_count, features = query_rows.shape
    blocks, blk, wide = key_value.shape
    side = fetched[0].shape[0]
    pool_rows = blocks + 4 * side
    slots = key_index.shape[1]
    lanes = 2 * features // HEADS
    pairs = HEADS // 2
    factor = 1.0 / math.sqrt(features // HEADS)
    row_spec = pl.BlockSpec((blk, lanes), lambda hp, b, *_: (b, hp))

    def kv_spec(count):
        return pl.BlockSpec((count, blk, 2 * lanes), lambda hp, b, *_: (0, 0, hp))

    return pl.pallas_call(
        functools.partial(attend_kernel, factor=factor),
        grid_spec=pltpu.PrefetchScalarGridSpec(
            num_scalar_prefetch=2,
            grid=(pairs, blocks),
            in_specs=[row_spec, row_spec, kv_spec(blocks)] + [kv_spec(side)] * 4,
            out_specs=[row_spec, row_spec, kv_spec(blocks), kv_spec(4 * side)],
            scratch_shapes=[
                pltpu.VMEM((pool_rows, blk, 2 * lanes), jnp.bfloat16),
                pltpu.VMEM((pool_rows, 2 * lanes, blk), jnp.bfloat16),
                pltpu.VMEM((pool_rows, blk, 2 * lanes), jnp.float32),
                pltpu.VMEM((slots, blk, blk), jnp.float32),
                pltpu.VMEM((slots, blk, blk), jnp.float32),
            ],
        ),
        out_shape=[
            jax.ShapeDtypeStruct((row_count, features), jnp.bfloat16),
            jax.ShapeDtypeStruct((row_count, features), jnp.bfloat16),
            jax.ShapeDtypeStruct((blocks, blk, wide), jnp.float32),
            jax.ShapeDtypeStruct((4 * side, blk, wide), jnp.bfloat16),
        ],
        compiler_params=pltpu.CompilerParams(
            dimension_semantics=("arbitrary", "arbitrary"), vmem_limit_bytes=48 << 20
        ),
        name="attend",
    )(key_index, live_keys, query_rows, d_context, key_value, *fetched)


def weave(left, right):
    rows, features = left.shape
    pairs = HEADS // 2
    both = jnp.stack(
        [left.reshape(rows, pairs, features // pairs), right.reshape(rows, pairs, features // pairs)],
        axis=2,
    )
    return both.reshape(rows, 2 * features)


def shards(
    tokens,
    norm_gain,
    w_query_key,
    w_value,
    w_out,
    cotangent,
    block_order,
    neighbour_ids,
    neighbour_count,
):
    row_count = tokens.shape[2]
    features = tokens.shape[3]
    blocks = row_count // BLK
    slot_count = neighbour_ids.shape[3]
    extent_x = lax.axis_size("bx")
    extent_y = lax.axis_size("by")
    brick_x = lax.axis_index("bx")
    brick_y = lax.axis_index("by")
    my_brick = brick_x * extent_y + brick_y
    row_order = block_order[0, 0]
    arrival_grad = cotangent[0, 0]
    values, inv_rms, arrival_normed = rms_rows(tokens[0, 0], norm_gain)
    order_mask = (
        row_order[:, None] == lax.broadcasted_iota(jnp.int32, (row_count, row_count), 1)
    ).astype(jnp.bfloat16)
    normed = jnp.dot(order_mask, arrival_normed, preferred_element_type=jnp.float32).astype(
        jnp.bfloat16
    )
    sorted_grad = jnp.dot(order_mask, arrival_grad, preferred_element_type=jnp.float32).astype(
        jnp.bfloat16
    )
    query_rows = jnp.dot(
        normed, w_query_key[:, :features], preferred_element_type=jnp.float32
    ).astype(jnp.bfloat16)
    w_pair = weave(w_query_key[:, features:], w_value)
    key_value = jnp.dot(normed, w_pair, preferred_element_type=jnp.float32).astype(jnp.bfloat16)
    key_value = key_value.reshape(blocks, BLK, 2 * features)
    d_context = lax.dot_general(
        sorted_grad, w_out, (((1,), (1,)), ((), ())), preferred_element_type=jnp.float32
    ).astype(jnp.bfloat16)
    slot_range = jnp.arange(slot_count, dtype=jnp.int32)
    block_range = jnp.arange(blocks, dtype=jnp.int32)
    side_range = jnp.arange(1, 5, dtype=jnp.int32)
    my_ids = neighbour_ids[brick_x, brick_y]
    my_count = neighbour_count[brick_x, brick_y]
    live_slots = slot_range[None, :] < my_count[:, None]
    owner_brick = my_ids // blocks
    offset = my_ids % blocks
    delta_x = owner_brick // extent_y - brick_x
    delta_y = owner_brick % extent_y - brick_y
    segment = jnp.where(
        delta_x == -1,
        1,
        jnp.where(delta_x == 1, 2, jnp.where(delta_y == -1, 3, jnp.where(delta_y == 1, 4, 0))),
    )

    def selection_for(req_x, req_y):
        safe_x = jnp.clip(req_x, 0, extent_x - 1)
        safe_y = jnp.clip(req_y, 0, extent_y - 1)
        req_ids = neighbour_ids[safe_x, safe_y]
        req_count = neighbour_count[safe_x, safe_y]
        req_live = slot_range[None, :] < req_count[:, None]
        from_me = req_live & (req_ids // blocks == my_brick)
        wanted = jnp.any(
            from_me[:, :, None] & ((req_ids % blocks)[:, :, None] == block_range), axis=(0, 1)
        )
        ranks = jnp.cumsum(wanted.astype(jnp.int32)) - 1
        pick_rows = wanted[None, :] & (ranks[None, :] == jnp.arange(CAP, dtype=jnp.int32)[:, None])
        return pick_rows.astype(jnp.bfloat16)

    choosers = {}
    for shift_step in (1, -1):
        choosers["bx", shift_step] = selection_for(brick_x + shift_step, brick_y)
        choosers["by", shift_step] = selection_for(brick_x, brick_y + shift_step)
    side_match = (segment[:, :, None, None] == side_range[None, None, :, None]) & (
        offset[:, :, None, None] == block_range[None, None, None, :]
    )
    wanted_here = jnp.any(live_slots[:, :, None, None] & side_match, axis=(0, 1))
    side_ranks = jnp.cumsum(wanted_here.astype(jnp.int32), axis=1) - 1
    rank_of = jnp.sum(jnp.where(side_match, side_ranks[None, None, :, :], 0), axis=(2, 3))
    entry_index = jnp.where(segment == 0, offset, blocks + (segment - 1) * CAP + rank_of)

    def outgoing(source, side_key):
        picked = jnp.einsum(
            "co,otf->ctf", choosers[side_key], source, preferred_element_type=jnp.float32
        )
        return picked.astype(jnp.bfloat16)

    def incoming(returned, side_key):
        return jnp.einsum(
            "co,ctf->otf", choosers[side_key], returned, preferred_element_type=jnp.float32
        )

    fetched = {}
    for shift_step in (1, -1):
        fetched["bx", shift_step] = from_behind(
            outgoing(key_value, ("bx", shift_step)), "bx", shift_step
        )
    for shift_step in (1, -1):
        fetched["by", shift_step] = from_behind(
            outgoing(key_value, ("by", shift_step)), "by", shift_step
        )
    key_index = jnp.concatenate([block_range[:, None], entry_index], axis=1)
    live_keys = jnp.concatenate([jnp.ones((blocks, 1), dtype=jnp.bool_), live_slots], axis=1)
    context, grad_query, own_grad, away_grad = attend(
        key_index,
        live_keys.astype(jnp.int32),
        query_rows,
        d_context,
        key_value,
        [fetched["bx", 1], fetched["bx", -1], fetched["by", 1], fetched["by", -1]],
    )
    returned = {}
    for index, (axis, shift_step) in enumerate((("bx", 1), ("bx", -1), ("by", 1), ("by", -1))):
        returned[axis, shift_step] = from_behind(
            away_grad[index * CAP : (index + 1) * CAP], axis, -shift_step
        )

    def unsort(rows):
        return lax.dot_general(
            order_mask, rows, (((0,), (0,)), ((), ())), preferred_element_type=jnp.float32
        ).astype(jnp.bfloat16)

    context = unsort(context)
    branch_out = jnp.dot(context, w_out, preferred_element_type=jnp.float32).astype(jnp.bfloat16)
    grad_out_part = lax.dot_general(
        context, arrival_grad, (((0,), (0,)), ((), ())), preferred_element_type=jnp.float32
    )
    grad_query = unsort(grad_query)
    grad_q_part = lax.dot_general(
        arrival_normed, grad_query, (((0,), (0,)), ((), ())), preferred_element_type=jnp.float32
    )
    grad_output, grad_q = lax.psum((grad_out_part, grad_q_part), ("bx", "by"))
    for side_key, rows in returned.items():
        own_grad = own_grad + incoming(rows, side_key)
    grad_kv = unsort(own_grad.astype(jnp.bfloat16).reshape(row_count, 2 * features))
    grad_normed = lax.dot_general(
        grad_query,
        w_query_key[:, :features],
        (((1,), (1,)), ((), ())),
        preferred_element_type=jnp.float32,
    ) + lax.dot_general(
        grad_kv, w_pair, (((1,), (1,)), ((), ())), preferred_element_type=jnp.float32
    )
    grad_kv_part = lax.dot_general(
        arrival_normed, grad_kv, (((0,), (0,)), ((), ())), preferred_element_type=jnp.float32
    )
    gain_part = jnp.sum(grad_normed * (values * inv_rms), axis=0)
    late_part = jnp.concatenate(
        [grad_kv_part, jnp.broadcast_to(gain_part[:, None], (features, 128))], axis=1
    )
    late_part, grad_output, grad_q = lax.optimization_barrier((late_part, grad_output, grad_q))
    late_sum = lax.psum(late_part, ("bx", "by"))
    grad_kv_sum = late_sum[:, : 2 * features]
    grad_gain = late_sum[:, 2 * features]
    scaled_grad = grad_normed * norm_gain
    grad_rows = inv_rms * scaled_grad - values * (inv_rms * inv_rms * inv_rms) * jnp.mean(
        values * scaled_grad, axis=-1, keepdims=True
    )
    pairs = HEADS // 2
    split = grad_kv_sum.reshape(features, pairs, 2, features // pairs)
    grad_key = split[:, :, 0].reshape(features, features)
    grad_val = split[:, :, 1].reshape(features, features)
    grad_qk = jnp.concatenate([grad_q, grad_key], axis=1)
    return (
        branch_out[None, None],
        grad_rows[None, None],
        grad_qk,
        grad_val,
        grad_output,
        grad_gain,
    )


def solution(mesh):
    placed = (
        P("bx", "by", None, None),
        P(),
        P(),
        P(),
        P(),
        P("bx", "by", None, None),
        P("bx", "by", None),
        P(),
        P(),
    )
    return jax.shard_map(
        shards,
        mesh=mesh,
        in_specs=placed,
        out_specs=(P("bx", "by", None, None), P("bx", "by", None, None), P(), P(), P(), P()),
        check_vma=False,
    )
```
